32 devices in a mesh: tx: 4 (over y, x), ty: 2 (over core), depth: 4 (over z).
Axes of the slice: x: 2, y: 2, z: 4, core: 2. Of those that a mesh axis runs over, the one named last changes fastest.
Arguments:
- volume: bfloat16 [128, 512, 512], P('depth', 'ty', 'tx'), may hold values from -6 to 6
- transfer: float32 [4, 2], replicated, may hold values from -1.5 to 1.5
- ray_start: int32 [4, 512, 512], P('depth', 'ty', 'tx'), may hold values from 0 to 15
- ray_stop: int32 [4, 512, 512], P('depth', 'ty', 'tx'), may hold values from 16 to 32
- pattern: int32 [4, 64, 4], P('depth', 'ty', 'tx'), may hold values 0 or 1
- depth_order: int32 [4], replicated, may hold values from 0 to 3, each once
Outputs:
- frame: float32 [4, 512, 512], P(None, 'ty', 'tx')
The draws below stay inside these ranges and needn't reach their ends.
Inputs may be any that keep to these rules, and one draw needn't show every extreme that they name: ray_start[s] < ray_stop[s] for every ray and slice. `depth_order`: each slice appears once.
All inputs are finite; a program needn't handle non-finite values. No bound on the sum of `pattern` on one device may be relied on, other than what follows from the above.
Results may differ from the reference program's by a relative error of at most 0.0003.
Values may be sent and summed in bfloat16 or wider, within the bound.
A program may use at most 64 MiB of HBM per device.

```python
import jax
import jax.numpy as jnp
from jax import lax

BZ = 32
NZ = 128
NY = 512
NX = 512
N_DEPTH = 4


def set_ends(result, key, least, top_value):
    spot = [jax.random.randint(jax.random.fold_in(key, axis), (), 0, length) for axis, length in enumerate(result.shape)]
    widest = result.shape.index(max(result.shape))
    neighbour = spot[:widest] + [(spot[widest] + 1) % result.shape[widest]] + spot[widest + 1:]
    return result.at[tuple(spot)].set(least).at[tuple(neighbour)].set(top_value)


def shard_levels(stream_key, shape, split, smallest, largest):
    loudness = 1.0
    for dim, shards_of in split:
        steps = jax.random.uniform(jax.random.fold_in(jax.random.fold_in(stream_key, 6), dim), (shards_of,), jnp.float32, smallest / len(split), largest / len(split))
        loudness = loudness * jnp.repeat(jnp.exp(steps), shape[dim] // shards_of).reshape((-1,) + (1,) * (len(shape) - 1 - dim))
    return loudness


def scatter_about(key, shape, scale, reach, split=(), kind=jnp.bfloat16):
    loudness = shard_levels(key, shape, split, -0.22, 0.18) if split else 1.0
    values = jax.random.normal(key, shape, jnp.float32) * scale * loudness
    return jnp.minimum(jnp.maximum(values, -reach), reach).astype(kind)


def setup_inputs(seed: int = 0) -> dict:
    splits = jax.random.split(jax.random.key(seed), 7)
    return {
        "volume": scatter_about(splits[0], (NZ, NY, NX), 1.0, 6.0, ((0, 4), (1, 2), (2, 4))),
        "transfer": jnp.clip(jax.random.uniform(splits[1], (4, 2), jnp.float32, -1.5, 1.5), -1.5, 1.5),
        "ray_start": set_ends(jax.random.randint(splits[2], (N_DEPTH, NY, NX), 0, BZ // 2), jax.random.fold_in(splits[2], 1), 0, (BZ // 2) - 1).astype(jnp.int32),
        "ray_stop": set_ends(jax.random.randint(splits[3], (N_DEPTH, NY, NX), BZ // 2, BZ + 1), jax.random.fold_in(splits[3], 1), BZ // 2, BZ).astype(jnp.int32),
        "pattern": set_ends((jax.random.randint(splits[4], (N_DEPTH, NY // 8, NX // 128), 0, 4) < 3).astype(jnp.int32), jax.random.fold_in(splits[4], 1), 0, 1),
        "depth_order": jax.random.permutation(splits[5], N_DEPTH).astype(jnp.int32),
    }


def local_partial(padded, transfer, ray_start, ray_stop, pattern, depth_count):
    samples = padded.shape[0] - 2
    values = padded[1:-1, 1:-1, 1:-1]
    grad_z = (padded[2:, 1:-1, 1:-1] - padded[:-2, 1:-1, 1:-1]) * 0.5
    grad_y = (padded[1:-1, 2:, 1:-1] - padded[1:-1, :-2, 1:-1]) * 0.5
    grad_x = (padded[1:-1, 1:-1, 2:] - padded[1:-1, 1:-1, :-2]) * 0.5
    lit = jnp.abs(0.48 * grad_x + 0.6 * grad_y + 0.64 * grad_z)
    shading = 0.3 + 0.7 * lit / jnp.sqrt(grad_x * grad_x + grad_y * grad_y + grad_z * grad_z + 1.0)
    rows_each = ray_start.shape[0] // pattern.shape[0]
    cols_each = ray_start.shape[1] // pattern.shape[1]
    pattern_full = jnp.repeat(jnp.repeat(pattern, rows_each, axis=0), cols_each, axis=1)
    layers = lax.broadcasted_iota(jnp.int32, (samples, 1, 1), 0)
    active = (layers >= ray_start[None]) & (layers < ray_stop[None]) & (pattern_full[None] > 0)
    density = jax.nn.softplus(transfer[3, 0] * values + transfer[3, 1]) * (2.0 / (samples * depth_count))
    opacity = jnp.where(active, 1.0 - jnp.exp(-density), jnp.float32(0.0))
    passed = jnp.cumprod(1.0 - opacity, axis=0)
    prior = jnp.concatenate([jnp.ones_like(passed[:1]), passed[:-1]], axis=0)
    weights = prior * opacity * shading
    tinted = jax.nn.sigmoid(transfer[:3, 0][:, None, None, None] * values[None] + transfer[:3, 1][:, None, None, None])
    colors = lax.optimization_barrier(jnp.sum(weights[None] * tinted, axis=1))
    return jnp.concatenate([colors, passed[-1][None]], axis=0)

def composite(partials, depth_order):
    count = partials.shape[0]

    def step(position, state_pair):
        colors, remain = state_pair
        slice_part = lax.dynamic_index_in_dim(partials, depth_order[position], 0, keepdims=False)
        return (colors + remain[None] * slice_part[:3], remain * slice_part[3])
    start_pair = (jnp.zeros(partials.shape[1:2 - 1 + 1][:0] + (3,) + partials.shape[2:], jnp.float32), jnp.ones(partials.shape[2:], jnp.float32))
    colors, remain = lax.fori_loop(0, count, step, start_pair)
    return jnp.concatenate([colors, 1.0 - remain[None]], axis=0)

def reference(volume, transfer, ray_start, ray_stop, pattern, depth_order):
    padz = jnp.pad(volume, ((1, 1), (0, 0), (0, 0)))

    def one_slice(slice_index):
        bricks = lax.dynamic_slice_in_dim(padz, slice_index * BZ, BZ + 2, 0).astype(jnp.float32)
        bricks = jnp.pad(bricks, ((0, 0), (1, 1), (1, 1)))
        return local_partial(bricks, transfer, ray_start[slice_index], ray_stop[slice_index], pattern[slice_index], N_DEPTH)
    partials = lax.map(one_slice, jnp.arange(N_DEPTH, dtype=jnp.int32))
    return composite(partials, depth_order)
```

```python
import functools
import math

import jax
import jax.numpy as jnp
from jax import lax
from jax.experimental import pallas as pl
from jax.experimental.pallas import tpu as pltpu
from jax.sharding import PartitionSpec as P

MESH = pl.DeviceIdType.MESH
ROWS = 16
LAG = 5
UNROLL = 8
LOG2E = math.log2(math.e)


def band(length, across):
    r = lax.broadcasted_iota(jnp.int32, (length, length), 0)
    c = lax.broadcasted_iota(jnp.int32, (length, length), 1)
    up, down = (r == c + 1, r + 1 == c) if across else (c == r + 1, c + 1 == r)
    return (up.astype(jnp.float32) - down.astype(jnp.float32)).astype(jnp.bfloat16)


def dot(a, b):
    return jnp.dot(a, b, preferred_element_type=jnp.float32)


def kernel(
    n, n_tx, n_ty, scale,
    vol, start_hbm, stop_hbm, pattern, transfer, order, out,
    vb, start, stop, yup, ydn, edge, xl, xr, gx, gy, dy, part, parts, fin,
    load_sem, halo_send, halo_recv, part_send, part_recv, fin_send, fin_recv,
):
    samples, ny, nx = vol.shape
    half = ny // 2
    chunks = ny // ROWS
    owned = chunks // n
    tx, ty, me = lax.axis_index("tx"), lax.axis_index("ty"), lax.axis_index("depth")

    loads = [
        pltpu.make_async_copy(vol, vb.at[pl.ds(1, samples)], load_sem.at[0]),
        pltpu.make_async_copy(start_hbm.at[0], start, load_sem.at[1]),
        pltpu.make_async_copy(stop_hbm.at[0], stop, load_sem.at[2]),
    ]
    for load in loads:
        load.start()

    barrier = pltpu.get_barrier_semaphore()
    for rel in range(1, n):
        pl.semaphore_signal(barrier, inc=1, device_id={"depth": lax.rem(me + rel, n)}, device_id_type=MESH)
    sides = (("tx", tx, n_tx), ("ty", ty, n_ty))
    expected = n - 1
    for axis, at, count in sides:
        @pl.when(at > 0)
        def _(axis=axis, at=at):
            pl.semaphore_signal(barrier, inc=1, device_id={axis: at - 1}, device_id_type=MESH)

        @pl.when(at < count - 1)
        def _(axis=axis, at=at):
            pl.semaphore_signal(barrier, inc=1, device_id={axis: at + 1}, device_id_type=MESH)

        expected = expected + jnp.where(at > 0, 1, 0) + jnp.where(at < count - 1, 1, 0)
    pl.semaphore_wait(barrier, expected)

    def shift(slot, axis, at, count, source, target, upward):
        return pltpu.make_async_remote_copy(
            src_ref=source, dst_ref=target, send_sem=halo_send.at[slot], recv_sem=halo_recv.at[slot],
            device_id={axis: at + 1 if upward else at - 1}, device_id_type=MESH,
        )

    last, first = pl.ds(ny - ROWS, ROWS), pl.ds(0, ROWS)
    halos = [
        (shift(0, "depth", me, n, vb.at[samples], vb.at[0], True), me, n, True, lambda: vb.at[0]),
        (shift(1, "depth", me, n, vb.at[1], vb.at[samples + 1], False), me, n, False, lambda: vb.at[samples + 1]),
        (shift(2, "ty", ty, n_ty, vb.at[pl.ds(1, samples), last], yup, True), ty, n_ty, True, lambda: yup),
        (shift(3, "ty", ty, n_ty, vb.at[pl.ds(1, samples), first], ydn, False), ty, n_ty, False, lambda: ydn),
        (shift(4, "tx", tx, n_tx, edge, xl, True), tx, n_tx, True, lambda: xl),
        (shift(5, "tx", tx, n_tx, edge, xr, False), tx, n_tx, False, lambda: xr),
    ]

    def send_halo(entry):
        copy, at, count, upward, place = entry
        pl.when(at < count - 1 if upward else at > 0)(copy.start)

        @pl.when(at == 0 if upward else at == count - 1)
        def _():
            place()[...] = jnp.zeros(place().shape, jnp.bfloat16)

    loads[0].wait()
    for entry in halos[:4]:
        send_halo(entry)

    group = 4
    r = lax.broadcasted_iota(jnp.int32, (nx, nx), 0)
    c = lax.broadcasted_iota(jnp.int32, (nx, nx), 1)

    def gather(step, total):
        z0 = step * group
        for k in range(group):
            hit = ((r == 0) & (c == z0 + k)) | ((r == nx - 1) & (c == samples + z0 + k))
            total = total + dot(vb[1 + z0 + k], hit.astype(jnp.float32).astype(jnp.bfloat16))
        return total

    columns = lax.fori_loop(0, samples // group, gather, jnp.zeros((ny, nx), jnp.float32))
    edge[...] = (columns[:half] + pltpu.roll(columns[half:], nx // 2, 1)).astype(jnp.bfloat16)
    for entry in halos[4:]:
        send_halo(entry)

    dy[...] = band(ny, False)

    @pl.loop(0, samples)
    def _(z):
        gy[z] = dot(dy[...], vb[1 + z])

    for copy, at, count, upward, place in halos:
        pl.when(at < count - 1 if upward else at > 0)(copy.wait_send)
        pl.when(at > 0 if upward else at < count - 1)(copy.wait_recv)

    lane = lax.broadcasted_iota(jnp.int32, (half, nx), 1)
    from_left = lax.rem(lane, nx // 2) >= samples
    held = jnp.where(from_left, xl[...].astype(jnp.float32), xr[...].astype(jnp.float32)).astype(jnp.bfloat16)
    dx = band(nx, True)
    row = lax.broadcasted_iota(jnp.int32, (ROWS, nx), 0)

    @pl.loop(0, samples)
    def _(z):
        for h in range(2):
            base = h * (nx // 2) + z
            low = ((r == base + samples) & (c == 0)).astype(jnp.float32)
            high = ((r == base) & (c == nx - 1)).astype(jnp.float32)
            rows = pl.ds(h * half, half)
            both = jnp.concatenate([vb[1 + z, rows], held], axis=1)
            weights = jnp.concatenate([dx, (high - low).astype(jnp.bfloat16)], axis=0)
            gx[z, rows] = dot(both, weights)
        above = pltpu.roll(yup[z].astype(jnp.float32), 1, 0)
        gy[z, first] = gy[z, first] - jnp.where(row == 0, above, 0.0)
        below = pltpu.roll(ydn[z].astype(jnp.float32), ROWS - 1, 0)
        gy[z, last] = gy[z, last] + jnp.where(row == ROWS - 1, below, 0.0)

    loads[1].wait()
    loads[2].wait()
    rows_each = ny // pattern.shape[1]
    slopes = [transfer[i, 0] * 0.5 for i in range(3)]
    offsets = [transfer[i, 1] * 0.5 for i in range(3)]
    slope, offset = transfer[3, 0] * LOG2E, transfer[3, 1] * LOG2E

    rank = [sum(jnp.where(order[q] == s, q, 0) for q in range(n)) for s in range(n)]
    before = [[jnp.where(rank[a] < rank[b], 1.0, 0.0) for b in range(n)] for a in range(n)]

    def part_copy(j, k, owner):
        return pltpu.make_async_remote_copy(
            src_ref=part.at[j], dst_ref=parts.at[me, k],
            send_sem=part_send.at[j], recv_sem=part_recv.at[me, k],
            device_id={"depth": owner}, device_id_type=MESH,
        )

    def fin_copy(j, k, rel):
        return pltpu.make_async_remote_copy(
            src_ref=fin.at[k], dst_ref=out.at[:, pl.ds(pl.multiple_of(j * ROWS, ROWS), ROWS)],
            send_sem=fin_send.at[k, rel - 1], recv_sem=fin_recv.at[j],
            device_id={"depth": lax.rem(me + rel, n)}, device_id_type=MESH,
        )

    def render(j):
        r0 = pl.multiple_of(j * ROWS, ROWS)
        rows = pl.ds(r0, ROWS)
        begin = start[rows]
        end = stop[rows]
        blocks = []
        for b in range(ROWS // rows_each):
            on = pattern[0, j * (ROWS // rows_each) + b, 0]
            blocks.append(jnp.where(on > 0, end[b * rows_each:(b + 1) * rows_each], 0))
        end = jnp.concatenate(blocks, axis=0)

        def layer(z, state):
            previous, v, passed, total, red, green, blue = state
            after = vb[z + 2, rows].astype(jnp.float32)
            dz = after - previous
            dyv, dxv = gy[z, rows], gx[z, rows]
            lit = jnp.abs(0.168 * dxv + 0.21 * dyv + 0.224 * dz)
            shade = 0.15 + lit * lax.rsqrt(dxv * dxv + dyv * dyv + dz * dz + 4.0)
            log = jnp.log(1.0 + jnp.exp2(v * slope + offset))
            through = jnp.exp2(log * (-scale * LOG2E))
            active = (begin <= z) & (end > z)
            now = jnp.where(active, passed * through, passed)
            weight = (passed - now) * shade
            tints = [jnp.tanh(v * slopes[i] + offsets[i]) for i in range(3)]
            return (
                v, after, now, total + weight,
                red + weight * tints[0], green + weight * tints[1], blue + weight * tints[2],
            )

        zero = jnp.zeros((ROWS, nx), jnp.float32)
        state = (
            vb[0, rows].astype(jnp.float32), vb[1, rows].astype(jnp.float32),
            jnp.ones((ROWS, nx), jnp.float32), zero, zero, zero, zero,
        )
        _, _, passed, total, red, green, blue = lax.fori_loop(0, samples, layer, state, unroll=UNROLL)
        values = (red + total, green + total, blue + total, 1.0 - passed)
        owner, k = lax.rem(j, n), j // n

        @pl.when(owner == me)
        def _():
            for i in range(4):
                parts[me, k, i] = values[i]

        @pl.when(owner != me)
        def _():
            for i in range(4):
                part[j, i] = values[i]
            part_copy(j, k, owner).start()

    def merge(j):
        owner, k = lax.rem(j, n), j // n

        @pl.when(owner == me)
        def _():
            for rel in range(1, n):
                source = lax.rem(me + rel, n)
                pltpu.make_async_remote_copy(
                    src_ref=part.at[j], dst_ref=parts.at[source, k],
                    send_sem=part_send.at[j], recv_sem=part_recv.at[source, k],
                    device_id={"depth": source}, device_id_type=MESH,
                ).wait_recv()
            hidden = [parts[s, k, 3] for s in range(n)]
            remain = 1.0 - hidden[0]
            for s in range(1, n):
                remain = remain * (1.0 - hidden[s])
            colors = [jnp.zeros_like(remain)] * 3
            for s in range(n):
                prefix = jnp.ones_like(remain)
                for a in range(n):
                    if a != s:
                        prefix = prefix * (1.0 - hidden[a] * before[a][s])
                colors = [colors[i] + prefix * parts[s, k, i] for i in range(3)]
            rows = pl.ds(pl.multiple_of(j * ROWS, ROWS), ROWS)
            for i, value in enumerate(colors + [1.0 - remain]):
                fin[k, i] = value
                out[i, rows] = value
            for rel in range(1, n):
                fin_copy(j, k, rel).start()

    @pl.loop(0, chunks + LAG)
    def _(j):
        pl.when(j < chunks)(lambda: render(j))
        pl.when(j >= LAG)(lambda: merge(j - LAG))

    @pl.loop(0, chunks)
    def _(j):
        owner, k = lax.rem(j, n), j // n

        @pl.when(owner == me)
        def _():
            for rel in range(1, n):
                fin_copy(j, k, rel).wait_send()

        @pl.when(owner != me)
        def _():
            part_copy(j, k, owner).wait_send()
            fin_copy(j, k, 1).wait_recv()


def solution(mesh):
    n, n_tx, n_ty = mesh.shape["depth"], mesh.shape["tx"], mesh.shape["ty"]

    def shards(volume, transfer, ray_start, ray_stop, pattern, depth_order):
        samples, ny, nx = volume.shape
        chunks = ny // ROWS
        owned = chunks // n
        f32, bf16 = jnp.float32, jnp.bfloat16
        any_space = pl.BlockSpec(memory_space=pl.ANY)
        smem = pl.BlockSpec(memory_space=pltpu.SMEM)
        dma = pltpu.SemaphoreType.DMA
        return pl.pallas_call(
            functools.partial(kernel, n, n_tx, n_ty, 2.0 / (samples * n)),
            out_shape=jax.ShapeDtypeStruct((4, ny, nx), f32),
            in_specs=[any_space, any_space, any_space, smem, smem, smem],
            out_specs=pl.BlockSpec(memory_space=pltpu.VMEM),
            scratch_shapes=[
                pltpu.VMEM((samples + 2, ny, nx), bf16),
                pltpu.VMEM((ny, nx), jnp.int32),
                pltpu.VMEM((ny, nx), jnp.int32),
                pltpu.VMEM((samples, ROWS, nx), bf16),
                pltpu.VMEM((samples, ROWS, nx), bf16),
                pltpu.VMEM((ny // 2, nx), bf16),
                pltpu.VMEM((ny // 2, nx), bf16),
                pltpu.VMEM((ny // 2, nx), bf16),
                pltpu.VMEM((samples, ny, nx), f32),
                pltpu.VMEM((samples, ny, nx), f32),
                pltpu.VMEM((ny, ny), bf16),
                pltpu.VMEM((chunks, 4, ROWS, nx), f32),
                pltpu.VMEM((n, owned, 4, ROWS, nx), f32),
                pltpu.VMEM((owned, 4, ROWS, nx), f32),
                dma((3,)), dma((6,)), dma((6,)),
                dma((chunks,)), dma((n, owned)), dma((owned, n - 1)), dma((chunks,)),
            ],
            compiler_params=pltpu.CompilerParams(
                collective_id=0, has_side_effects=True, vmem_limit_bytes=40 * 1024 * 1024
            ),
        )(volume, ray_start, ray_stop, pattern, transfer, depth_order)

    in_specs = (
        P("depth", "ty", "tx"),
        P(),
        P("depth", "ty", "tx"),
        P("depth", "ty", "tx"),
        P("depth", "ty", "tx"),
        P(),
    )
    return jax.shard_map(shards, mesh=mesh, in_specs=in_specs, out_specs=P(None, "ty", "tx"), check_vma=False)
```

```python
import functools
import math

import jax
import jax.numpy as jnp
from jax import lax
from jax.experimental import pallas as pl
from jax.experimental.pallas import tpu as pltpu
from jax.sharding import PartitionSpec as P

MESH = pl.DeviceIdType.MESH
ROWS = 16
LAG = 5
UNROLL = 8
LOG2E = math.log2(math.e)
OCTAVES = 22
CODES = 65535.0 / OCTAVES


def encode(x):
    place = jnp.log(jnp.clip(x, 1e-30, 1.0)) * (CODES * LOG2E) + 65535.5
    return (jnp.maximum(place, 0.0).astype(jnp.int32) - 32768).astype(jnp.int16)


def decode(code):
    wide = code.astype(jnp.int32)
    value = jnp.exp2((wide.astype(jnp.float32) - 32767.0) * (1.0 / CODES))
    return jnp.where(wide == -32768, 0.0, value)


def dot(a, b):
    return jnp.dot(a, b, preferred_element_type=jnp.float32)


def kernel(
    n, n_tx, n_ty, scale,
    vol, start_hbm, stop_hbm, pattern, transfer, order, out,
    vb, start, stop, yup, ydn, edge, xl, xr, vf, held, part, parts, fin,
    load_sem, halo_send, halo_recv, part_send, part_recv, fin_send, fin_recv,
):
    samples, ny, nx = vol.shape
    half = ny // 2
    chunks = ny // ROWS
    owned = chunks // n
    tx, ty, me = lax.axis_index("tx"), lax.axis_index("ty"), lax.axis_index("depth")

    loads = [
        pltpu.make_async_copy(vol, vb.at[pl.ds(1, samples)], load_sem.at[0]),
        pltpu.make_async_copy(start_hbm.at[0], start, load_sem.at[1]),
        pltpu.make_async_copy(stop_hbm.at[0], stop, load_sem.at[2]),
    ]
    for load in loads:
        load.start()

    barrier = pltpu.get_barrier_semaphore()
    for rel in range(1, n):
        pl.semaphore_signal(barrier, inc=1, device_id={"depth": lax.rem(me + rel, n)}, device_id_type=MESH)
    sides = (("tx", tx, n_tx), ("ty", ty, n_ty))
    expected = n - 1
    for axis, at, count in sides:
        @pl.when(at > 0)
        def _(axis=axis, at=at):
            pl.semaphore_signal(barrier, inc=1, device_id={axis: at - 1}, device_id_type=MESH)

        @pl.when(at < count - 1)
        def _(axis=axis, at=at):
            pl.semaphore_signal(barrier, inc=1, device_id={axis: at + 1}, device_id_type=MESH)

        expected = expected + jnp.where(at > 0, 1, 0) + jnp.where(at < count - 1, 1, 0)
    pl.semaphore_wait(barrier, expected)

    def shift(slot, axis, at, count, source, target, upward):
        return pltpu.make_async_remote_copy(
            src_ref=source, dst_ref=target, send_sem=halo_send.at[slot], recv_sem=halo_recv.at[slot],
            device_id={axis: at + 1 if upward else at - 1}, device_id_type=MESH,
        )

    last, first = pl.ds(ny - ROWS, ROWS), pl.ds(0, ROWS)
    halos = [
        (shift(0, "depth", me, n, vb.at[samples], vb.at[0], True), me, n, True, lambda: vb.at[0]),
        (shift(1, "depth", me, n, vb.at[1], vb.at[samples + 1], False), me, n, False, lambda: vb.at[samples + 1]),
        (shift(2, "ty", ty, n_ty, vb.at[pl.ds(1, samples), last], yup, True), ty, n_ty, True, lambda: yup),
        (shift(3, "ty", ty, n_ty, vb.at[pl.ds(1, samples), first], ydn, False), ty, n_ty, False, lambda: ydn),
        (shift(4, "tx", tx, n_tx, edge, xl, True), tx, n_tx, True, lambda: xl),
        (shift(5, "tx", tx, n_tx, edge, xr, False), tx, n_tx, False, lambda: xr),
    ]

    def send_halo(entry):
        copy, at, count, upward, place = entry
        pl.when(at < count - 1 if upward else at > 0)(copy.start)

        @pl.when(at == 0 if upward else at == count - 1)
        def _():
            place()[...] = jnp.zeros(place().shape, jnp.bfloat16)

    loads[0].wait()
    for entry in halos[:4]:
        send_halo(entry)

    group = 4
    r = lax.broadcasted_iota(jnp.int32, (nx, nx), 0)
    c = lax.broadcasted_iota(jnp.int32, (nx, nx), 1)

    def gather(step, total):
        z0 = step * group
        for k in range(group):
            lane = 2 * (z0 + k)
            hit = ((r == nx - 1) & (c == lane)) | ((r == 0) & (c == lax.rem(lane + nx - 1, nx)))
            total = total + dot(vb[1 + z0 + k], hit.astype(jnp.float32).astype(jnp.bfloat16))
        return total

    columns = lax.fori_loop(0, samples // group, gather, jnp.zeros((ny, nx), jnp.float32))
    edge[...] = (columns[:half] + pltpu.roll(columns[half:], nx // 2, 1)).astype(jnp.bfloat16)
    for entry in halos[4:]:
        send_halo(entry)

    body = pl.ds(8, ny)

    @pl.loop(0, samples)
    def _(z):
        vf[1 + z, body] = vb[1 + z].astype(jnp.float32)

    for copy, at, count, upward, place in halos:
        pl.when(at < count - 1 if upward else at > 0)(copy.wait_send)
        pl.when(at > 0 if upward else at < count - 1)(copy.wait_recv)

    lane = lax.broadcasted_iota(jnp.int32, (half, nx), 1)
    held[...] = jnp.where(lax.rem(lane, 2) == 0, xl[...].astype(jnp.float32), xr[...].astype(jnp.float32))
    for z in (0, samples + 1):
        vf[z, body] = vb[z].astype(jnp.float32)

    @pl.loop(0, samples)
    def _(z):
        vf[1 + z, pl.ds(0, 8)] = yup[z].astype(jnp.float32)[ROWS - 8:]
        vf[1 + z, pl.ds(8 + ny, 8)] = ydn[z].astype(jnp.float32)[:8]

    loads[1].wait()
    loads[2].wait()
    rows_each = ny // pattern.shape[1]
    slopes = [transfer[0, i] * 0.5 for i in range(3)]
    offsets = [transfer[1, i] * 0.5 for i in range(3)]
    slope, offset = transfer[0, 3] * LOG2E, transfer[1, 3] * LOG2E

    rank = [sum(jnp.where(order[q] == s, q, 0) for q in range(n)) for s in range(n)]
    before = [[jnp.where(rank[a] < rank[b], 1.0, 0.0) for b in range(n)] for a in range(n)]

    def part_copy(j, k, owner):
        return pltpu.make_async_remote_copy(
            src_ref=part.at[j], dst_ref=parts.at[me, k],
            send_sem=part_send.at[j], recv_sem=part_recv.at[me, k],
            device_id={"depth": owner}, device_id_type=MESH,
        )

    def fin_copy(j, k, rel):
        return pltpu.make_async_remote_copy(
            src_ref=fin.at[k], dst_ref=out.at[:, pl.ds(pl.multiple_of(j * ROWS, ROWS), ROWS)],
            send_sem=fin_send.at[k, rel - 1], recv_sem=fin_recv.at[j],
            device_id={"depth": lax.rem(me + rel, n)}, device_id_type=MESH,
        )

    def render(j):
        r0 = pl.multiple_of(j * ROWS, ROWS)
        rows = pl.ds(r0, ROWS)
        begin = start[rows]
        end = stop[rows]
        blocks = []
        for b in range(ROWS // rows_each):
            on = pattern[0, j * (ROWS // rows_each) + b]
            blocks.append(jnp.where(on > 0, end[b * rows_each:(b + 1) * rows_each], 0))
        end = jnp.concatenate(blocks, axis=0)

        def layer(z, state):
            previous, v, passed, total, red, green, blue = state
            after = vf[z + 2, pl.ds(pl.multiple_of(r0 + 8, 8), ROWS)]
            near = vf.at[z + 1, pl.ds(r0, ROWS + 16)]
            dz = after - previous
            dyv = near[pl.ds(9, ROWS)] - near[pl.ds(7, ROWS)]
            beside = pltpu.roll(sides_of, lax.rem(nx - 2 * z, nx), 1)
            right = jnp.where(lane == nx - 1, beside, pltpu.roll(v, nx - 1, 1))
            dxv = right - jnp.where(lane == 0, beside, pltpu.roll(v, 1, 1))
            lit = jnp.abs(0.168 * dxv + 0.21 * dyv + 0.224 * dz)
            shade = 0.15 + lit * lax.rsqrt(dxv * dxv + dyv * dyv + dz * dz + 4.0)
            log = jnp.log(1.0 + jnp.exp2(v * slope + offset))
            through = jnp.exp2(log * (-scale * LOG2E))
            active = (begin <= z) & (end > z)
            now = jnp.where(active, passed * through, passed)
            weight = (passed - now) * shade
            tints = [jnp.tanh(v * slopes[i] + offsets[i]) for i in range(3)]
            return (
                v, after, now, total + weight,
                red + weight * tints[0], green + weight * tints[1], blue + weight * tints[2],
            )

        upper = j * ROWS // half
        sides_of = held[pl.ds(pl.multiple_of(r0 - upper * half, ROWS), ROWS)]
        sides_of = pltpu.roll(sides_of, upper * (nx // 2), 1)
        lane = lax.broadcasted_iota(jnp.int32, (ROWS, nx), 1)
        zero = jnp.zeros((ROWS, nx), jnp.float32)
        inner = pl.ds(pl.multiple_of(r0 + 8, 8), ROWS)
        state = (
            vf[0, inner], vf[1, inner],
            jnp.ones((ROWS, nx), jnp.float32), zero, zero, zero, zero,
        )
        _, _, passed, total, red, green, blue = lax.fori_loop(0, samples, layer, state, unroll=UNROLL)
        values = [encode(x) for x in (red + total, green + total, blue + total, 1.0 - passed)]
        owner, k = lax.rem(j, n), j // n

        @pl.when(owner == me)
        def _():
            for i in range(4):
                parts[me, k, i] = values[i]

        @pl.when(owner != me)
        def _():
            for i in range(4):
                part[j, i] = values[i]
            part_copy(j, k, owner).start()

    def merge(j):
        owner, k = lax.rem(j, n), j // n

        @pl.when(owner == me)
        def _():
            for rel in range(1, n):
                source = lax.rem(me + rel, n)
                pltpu.make_async_remote_copy(
                    src_ref=part.at[j], dst_ref=parts.at[source, k],
                    send_sem=part_send.at[j], recv_sem=part_recv.at[source, k],
                    device_id={"depth": source}, device_id_type=MESH,
                ).wait_recv()
            hidden = [decode(parts[s, k, 3]) for s in range(n)]
            remain = 1.0 - hidden[0]
            for s in range(1, n):
                remain = remain * (1.0 - hidden[s])
            colors = [jnp.zeros_like(remain)] * 3
            for s in range(n):
                prefix = jnp.ones_like(remain)
                for a in range(n):
                    if a != s:
                        prefix = prefix * (1.0 - hidden[a] * before[a][s])
                colors = [colors[i] + prefix * decode(parts[s, k, i]) for i in range(3)]
            rows = pl.ds(pl.multiple_of(j * ROWS, ROWS), ROWS)
            for i, value in enumerate(colors + [1.0 - remain]):
                fin[k, i] = encode(value)
                out[i, rows] = encode(value)
            for rel in range(1, n):
                fin_copy(j, k, rel).start()

    @pl.loop(0, chunks + LAG)
    def _(j):
        pl.when(j < chunks)(lambda: render(j))
        pl.when(j >= LAG)(lambda: merge(j - LAG))

    @pl.loop(0, chunks)
    def _(j):
        owner, k = lax.rem(j, n), j // n

        @pl.when(owner == me)
        def _():
            for rel in range(1, n):
                fin_copy(j, k, rel).wait_send()

        @pl.when(owner != me)
        def _():
            part_copy(j, k, owner).wait_send()
            fin_copy(j, k, 1).wait_recv()


def solution(mesh):
    n, n_tx, n_ty = mesh.shape["depth"], mesh.shape["tx"], mesh.shape["ty"]

    def shards(volume, transfer, ray_start, ray_stop, pattern, depth_order):
        samples, ny, nx = volume.shape
        chunks = ny // ROWS
        owned = chunks // n
        f32, bf16, i16 = jnp.float32, jnp.bfloat16, jnp.int16
        any_space = pl.BlockSpec(memory_space=pl.ANY)
        smem = pl.BlockSpec(memory_space=pltpu.SMEM)
        dma = pltpu.SemaphoreType.DMA
        codes = pl.pallas_call(
            functools.partial(kernel, n, n_tx, n_ty, 2.0 / (samples * n)),
            out_shape=jax.ShapeDtypeStruct((4, ny, nx), i16),
            in_specs=[any_space, any_space, any_space, smem, smem, smem],
            out_specs=pl.BlockSpec(memory_space=pltpu.VMEM),
            scratch_shapes=[
                pltpu.VMEM((samples + 2, ny, nx), bf16),
                pltpu.VMEM((ny, nx), jnp.int32),
                pltpu.VMEM((ny, nx), jnp.int32),
                pltpu.VMEM((samples, ROWS, nx), bf16),
                pltpu.VMEM((samples, ROWS, nx), bf16),
                pltpu.VMEM((ny // 2, nx), bf16),
                pltpu.VMEM((ny // 2, nx), bf16),
                pltpu.VMEM((ny // 2, nx), bf16),
                pltpu.VMEM((samples + 2, ny + 16, nx), f32),
                pltpu.VMEM((ny // 2, nx), f32),
                pltpu.VMEM((chunks, 4, ROWS, nx), i16),
                pltpu.VMEM((n, owned, 4, ROWS, nx), i16),
                pltpu.VMEM((owned, 4, ROWS, nx), i16),
                dma((3,)), dma((6,)), dma((6,)),
                dma((chunks,)), dma((n, owned)), dma((owned, n - 1)), dma((chunks,)),
            ],
            compiler_params=pltpu.CompilerParams(
                collective_id=0, has_side_effects=True, vmem_limit_bytes=62 * 1024 * 1024
            ),
        )(volume, ray_start, ray_stop, pattern[:, :, 0], transfer.T, depth_order)
        return decode(codes)

    in_specs = (
        P("depth", "ty", "tx"),
        P(),
        P("depth", "ty", "tx"),
        P("depth", "ty", "tx"),
        P("depth", "ty", "tx"),
        P(),
    )
    return jax.shard_map(shards, mesh=mesh, in_specs=in_specs, out_specs=P(None, "ty", "tx"), check_vma=False)
```

```python
import functools
import math

import jax
import jax.numpy as jnp
from jax import lax
from jax.experimental import pallas as pl
from jax.experimental.pallas import tpu as pltpu
from jax.sharding import PartitionSpec as P

MESH = pl.DeviceIdType.MESH
STRIP = 16
LAG_ROWS = 224
UNROLL = 16
LOG2E = math.log2(math.e)
OCTAVES = 22
CODES = 65535.0 / OCTAVES


def encode(x):
    place = jnp.log(jnp.clip(x, 1e-30, 1.0)) * (CODES * LOG2E) + 65535.5
    return (jnp.maximum(place, 0.0).astype(jnp.int32) - 32768).astype(jnp.int16)


def decode(code):
    wide = code.astype(jnp.int32)
    value = jnp.exp2((wide.astype(jnp.float32) - 32767.0) * (1.0 / CODES))
    return jnp.where(wide == -32768, 0.0, value)


def dot(a, b):
    return jnp.dot(a, b, preferred_element_type=jnp.float32)


def kernel(
    n, n_tx, n_ty, scale, each,
    vol, start_hbm, stop_hbm, pattern, transfer, order, out,
    vb, start, stop, yup, ydn, edge, xl, xr, vf, share, held, part, parts, fin,
    load_sem, halo_send, halo_recv, part_send, part_recv, fin_send, fin_recv,
):
    samples, ny, nx = vol.shape
    half = ny // 2
    chunks = ny // each
    lag = LAG_ROWS // each
    tx, ty, me = lax.axis_index("tx"), lax.axis_index("ty"), lax.axis_index("depth")

    loads = [
        pltpu.make_async_copy(vol, vb.at[pl.ds(1, samples)], load_sem.at[0]),
        pltpu.make_async_copy(start_hbm.at[0], start, load_sem.at[1]),
        pltpu.make_async_copy(stop_hbm.at[0], stop, load_sem.at[2]),
    ]
    for load in loads:
        load.start()

    barrier = pltpu.get_barrier_semaphore()
    for rel in range(1, n):
        pl.semaphore_signal(barrier, inc=1, device_id={"depth": lax.rem(me + rel, n)}, device_id_type=MESH)
    sides = (("tx", tx, n_tx), ("ty", ty, n_ty))
    expected = n - 1
    for axis, at, count in sides:
        @pl.when(at > 0)
        def _(axis=axis, at=at):
            pl.semaphore_signal(barrier, inc=1, device_id={axis: at - 1}, device_id_type=MESH)

        @pl.when(at < count - 1)
        def _(axis=axis, at=at):
            pl.semaphore_signal(barrier, inc=1, device_id={axis: at + 1}, device_id_type=MESH)

        expected = expected + jnp.where(at > 0, 1, 0) + jnp.where(at < count - 1, 1, 0)
    pl.semaphore_wait(barrier, expected)

    def shift(slot, axis, at, count, source, target, upward):
        return pltpu.make_async_remote_copy(
            src_ref=source, dst_ref=target, send_sem=halo_send.at[slot], recv_sem=halo_recv.at[slot],
            device_id={axis: at + 1 if upward else at - 1}, device_id_type=MESH,
        )

    last, first = pl.ds(ny - STRIP, STRIP), pl.ds(0, STRIP)
    halos = [
        (shift(0, "depth", me, n, vb.at[samples], vb.at[0], True), me, n, True, lambda: vb.at[0]),
        (shift(1, "depth", me, n, vb.at[1], vb.at[samples + 1], False), me, n, False, lambda: vb.at[samples + 1]),
        (shift(2, "ty", ty, n_ty, vb.at[pl.ds(1, samples), last], yup, True), ty, n_ty, True, lambda: yup),
        (shift(3, "ty", ty, n_ty, vb.at[pl.ds(1, samples), first], ydn, False), ty, n_ty, False, lambda: ydn),
        (shift(4, "tx", tx, n_tx, edge, xl, True), tx, n_tx, True, lambda: xl),
        (shift(5, "tx", tx, n_tx, edge, xr, False), tx, n_tx, False, lambda: xr),
    ]

    def send_halo(entry):
        copy, at, count, upward, place = entry
        pl.when(at < count - 1 if upward else at > 0)(copy.start)

        @pl.when(at == 0 if upward else at == count - 1)
        def _():
            place()[...] = jnp.zeros(place().shape, jnp.bfloat16)

    loads[0].wait()
    for entry in halos[:4]:
        send_halo(entry)

    group = 4
    r = lax.broadcasted_iota(jnp.int32, (nx, nx), 0)
    c = lax.broadcasted_iota(jnp.int32, (nx, nx), 1)

    def gather(step, total):
        z0 = step * group
        hits = []
        for k in range(group):
            lane = 2 * (z0 + k)
            hit = ((r == nx - 1) & (c == lane)) | ((r == 0) & (c == lax.rem(lane + nx - 1, nx)))
            hits.append(hit.astype(jnp.float32).astype(jnp.bfloat16))
        layers = jnp.concatenate([vb[1 + z0 + k] for k in range(group)], axis=1)
        return total + dot(layers, jnp.concatenate(hits, axis=0))

    columns = lax.fori_loop(0, samples // group, gather, jnp.zeros((ny, nx), jnp.float32))
    edge[...] = (columns[:half] + pltpu.roll(columns[half:], nx // 2, 1)).astype(jnp.bfloat16)
    for entry in halos[4:]:
        send_halo(entry)

    body = pl.ds(8, ny)

    loads[1].wait()
    loads[2].wait()
    rows_each = ny // pattern.shape[1]
    slopes = [transfer[0, i] * 0.5 for i in range(3)]
    offsets = [transfer[1, i] * 0.5 for i in range(3)]
    slope, offset = transfer[0, 3] * LOG2E, transfer[1, 3] * LOG2E

    rank = [sum(jnp.where(order[q] == s, q, 0) for q in range(n)) for s in range(n)]
    before = [[jnp.where(rank[a] < rank[b], 1.0, 0.0) for b in range(n)] for a in range(n)]

    def owner_of(j):
        turn = lax.rem(j, n)
        return jnp.where(lax.rem(turn, 2) == 0, turn // 2, n - 1 - turn // 2)

    @pl.loop(0, chunks)
    def _(j):
        r0 = pl.multiple_of(j * each, each)
        rows, inner = pl.ds(r0, each), pl.ds(pl.multiple_of(r0 + 8, 8), each)
        begin = start[rows]
        end = stop[rows]
        blocks = []
        for b in range(each // rows_each):
            on = pattern[0, j * (each // rows_each) + b]
            blocks.append(jnp.where(on > 0, end[b * rows_each:(b + 1) * rows_each], 0))
        end = jnp.concatenate(blocks, axis=0)

        def layer(z, passed):
            v = vb[z + 1, rows].astype(jnp.float32)
            vf[z + 1, inner] = v
            log = jnp.log(1.0 + jnp.exp2(v * slope + offset))
            through = jnp.exp2(log * (-scale * LOG2E))
            active = (begin <= z) & (end > z)
            now = jnp.where(active, passed * through, passed)
            share[z, rows] = passed - now
            return now

        passed = lax.fori_loop(0, samples, layer, jnp.ones((each, nx), jnp.float32), unroll=UNROLL)
        hidden = encode(1.0 - passed)
        owner, k = owner_of(j), j // n

        @pl.when(owner == me)
        def _():
            parts[me, k, 3] = hidden

        @pl.when(owner != me)
        def _():
            part[j, 3] = hidden

    for copy, at, count, upward, place in halos:
        pl.when(at < count - 1 if upward else at > 0)(copy.wait_send)
        pl.when(at > 0 if upward else at < count - 1)(copy.wait_recv)

    lane = lax.broadcasted_iota(jnp.int32, (half, nx), 1)
    held[...] = jnp.where(lax.rem(lane, 2) == 0, xl[...].astype(jnp.float32), xr[...].astype(jnp.float32))
    for z in (0, samples + 1):
        vf[z, body] = vb[z].astype(jnp.float32)

    @pl.loop(0, samples)
    def _(z):
        vf[1 + z, pl.ds(0, 8)] = yup[z].astype(jnp.float32)[STRIP - 8:]
        vf[1 + z, pl.ds(8 + ny, 8)] = ydn[z].astype(jnp.float32)[:8]

    def part_copy(j, k, owner):
        return pltpu.make_async_remote_copy(
            src_ref=part.at[j], dst_ref=parts.at[me, k],
            send_sem=part_send.at[j], recv_sem=part_recv.at[me, k],
            device_id={"depth": owner}, device_id_type=MESH,
        )

    def fin_copy(j, k, rel):
        return pltpu.make_async_remote_copy(
            src_ref=fin.at[k], dst_ref=out.at[:, pl.ds(pl.multiple_of(j * each, each), each)],
            send_sem=fin_send.at[k, rel - 1], recv_sem=fin_recv.at[j],
            device_id={"depth": lax.rem(me + rel, n)}, device_id_type=MESH,
        )

    def render(j):
        r0 = pl.multiple_of(j * each, each)
        rows = pl.ds(r0, each)
        def layer(z, state):
            previous, v, total, red, green, blue = state
            after = vf[z + 2, pl.ds(pl.multiple_of(r0 + 8, 8), each)]
            near = vf.at[z + 1, pl.ds(r0, each + 16)]
            dz = after - previous
            dyv = near[pl.ds(9, each)] - near[pl.ds(7, each)]
            beside = pltpu.roll(sides_of, lax.rem(nx - 2 * z, nx), 1)
            right = jnp.where(lane == nx - 1, beside, pltpu.roll(v, nx - 1, 1))
            dxv = right - jnp.where(lane == 0, beside, pltpu.roll(v, 1, 1))
            lit = jnp.abs(0.168 * dxv + 0.21 * dyv + 0.224 * dz)
            shade = 0.15 + lit * lax.rsqrt(dxv * dxv + dyv * dyv + dz * dz + 4.0)
            weight = share[z, rows] * shade
            tints = [jnp.tanh(v * slopes[i] + offsets[i]) for i in range(3)]
            return (
                v, after, total + weight,
                red + weight * tints[0], green + weight * tints[1], blue + weight * tints[2],
            )

        upper = j * each // half
        sides_of = held[pl.ds(pl.multiple_of(r0 - upper * half, each), each)]
        sides_of = pltpu.roll(sides_of, upper * (nx // 2), 1)
        lane = lax.broadcasted_iota(jnp.int32, (each, nx), 1)
        zero = jnp.zeros((each, nx), jnp.float32)
        inner = pl.ds(pl.multiple_of(r0 + 8, 8), each)
        state = (
            vf[0, inner], vf[1, inner],
            zero, zero, zero, zero,
        )
        _, _, total, red, green, blue = lax.fori_loop(0, samples, layer, state, unroll=UNROLL)
        values = [encode(x) for x in (red + total, green + total, blue + total)]
        owner, k = owner_of(j), j // n

        @pl.when(owner == me)
        def _():
            for i in range(3):
                parts[me, k, i] = values[i]

        @pl.when(owner != me)
        def _():
            for i in range(3):
                part[j, i] = values[i]
            part_copy(j, k, owner).start()

    def merge(j):
        owner, k = owner_of(j), j // n

        @pl.when(owner == me)
        def _():
            for rel in range(1, n):
                source = lax.rem(me + rel, n)
                pltpu.make_async_remote_copy(
                    src_ref=part.at[j], dst_ref=parts.at[source, k],
                    send_sem=part_send.at[j], recv_sem=part_recv.at[source, k],
                    device_id={"depth": source}, device_id_type=MESH,
                ).wait_recv()
            hidden = [decode(parts[s, k, 3]) for s in range(n)]
            remain = 1.0 - hidden[0]
            for s in range(1, n):
                remain = remain * (1.0 - hidden[s])
            colors = [jnp.zeros_like(remain)] * 3
            for s in range(n):
                prefix = jnp.ones_like(remain)
                for a in range(n):
                    if a != s:
                        prefix = prefix * (1.0 - hidden[a] * before[a][s])
                colors = [colors[i] + prefix * decode(parts[s, k, i]) for i in range(3)]
            rows = pl.ds(pl.multiple_of(j * each, each), each)
            for i, value in enumerate(colors + [1.0 - remain]):
                fin[k, i] = encode(value)
                out[i, rows] = encode(value)
            for rel in range(1, n):
                fin_copy(j, k, rel).start()

    @pl.loop(0, chunks + lag)
    def _(j):
        pl.when(j < chunks)(lambda: render(j))
        pl.when(j >= lag)(lambda: merge(j - lag))

    @pl.loop(0, chunks)
    def _(j):
        owner, k = owner_of(j), j // n

        @pl.when(owner == me)
        def _():
            for rel in range(1, n):
                fin_copy(j, k, rel).wait_send()

        @pl.when(owner != me)
        def _():
            part_copy(j, k, owner).wait_send()
            fin_copy(j, k, 1).wait_recv()


def solution(mesh):
    n, n_tx, n_ty = mesh.shape["depth"], mesh.shape["tx"], mesh.shape["ty"]

    def shards(volume, transfer, ray_start, ray_stop, pattern, depth_order):
        samples, ny, nx = volume.shape
        rows = min(32, ny // n)
        chunks = ny // rows
        owned = chunks // n
        f32, bf16, i16 = jnp.float32, jnp.bfloat16, jnp.int16
        any_space = pl.BlockSpec(memory_space=pl.ANY)
        smem = pl.BlockSpec(memory_space=pltpu.SMEM)
        dma = pltpu.SemaphoreType.DMA
        codes = pl.pallas_call(
            functools.partial(kernel, n, n_tx, n_ty, 2.0 / (samples * n), rows),
            out_shape=jax.ShapeDtypeStruct((4, ny, nx), i16),
            in_specs=[any_space, any_space, any_space, smem, smem, smem],
            out_specs=pl.BlockSpec(memory_space=pltpu.VMEM),
            scratch_shapes=[
                pltpu.VMEM((samples + 2, ny, nx), bf16),
                pltpu.VMEM((ny, nx), jnp.int32),
                pltpu.VMEM((ny, nx), jnp.int32),
                pltpu.VMEM((samples, STRIP, nx), bf16),
                pltpu.VMEM((samples, STRIP, nx), bf16),
                pltpu.VMEM((ny // 2, nx), bf16),
                pltpu.VMEM((ny // 2, nx), bf16),
                pltpu.VMEM((ny // 2, nx), bf16),
                pltpu.VMEM((samples + 2, ny + 16, nx), f32),
                pltpu.VMEM((samples, ny, nx), f32),
                pltpu.VMEM((ny // 2, nx), f32),
                pltpu.VMEM((chunks, 4, rows, nx), i16),
                pltpu.VMEM((n, owned, 4, rows, nx), i16),
                pltpu.VMEM((owned, 4, rows, nx), i16),
                dma((3,)), dma((6,)), dma((6,)),
                dma((chunks,)), dma((n, owned)), dma((owned, n - 1)), dma((chunks,)),
            ],
            compiler_params=pltpu.CompilerParams(
                collective_id=0, has_side_effects=True, vmem_limit_bytes=62 * 1024 * 1024
            ),
        )(volume, ray_start, ray_stop, pattern[:, :, 0], transfer.T, depth_order)
        return decode(codes)

    in_specs = (
        P("depth", "ty", "tx"),
        P(),
        P("depth", "ty", "tx"),
        P("depth", "ty", "tx"),
        P("depth", "ty", "tx"),
        P(),
    )
    return jax.shard_map(shards, mesh=mesh, in_specs=in_specs, out_specs=P(None, "ty", "tx"), check_vma=False)
```

```python
import functools
import math

import jax
import jax.numpy as jnp
from jax import lax
from jax.experimental import pallas as pl
from jax.experimental.pallas import tpu as pltpu
from jax.sharding import PartitionSpec as P

MESH = pl.DeviceIdType.MESH
STRIP = 16
LAG_ROWS = 224
UNROLL = 32
LOG2E = math.log2(math.e)
OCTAVES = 22
CODES = 65535.0 / OCTAVES


def encode(x):
    place = jnp.log(jnp.clip(x, 1e-30, 1.0)) * (CODES * LOG2E) + 65535.5
    return (jnp.maximum(place, 0.0).astype(jnp.int32) - 32768).astype(jnp.int16)


def decode(code):
    wide = code.astype(jnp.int32)
    value = jnp.exp2((wide.astype(jnp.float32) - 32767.0) * (1.0 / CODES))
    return jnp.where(wide == -32768, 0.0, value)


def dot(a, b):
    return jnp.dot(a, b, preferred_element_type=jnp.float32)


def kernel(
    n, n_tx, n_ty, scale, each,
    vol, start_hbm, stop_hbm, pattern, transfer, order, out,
    vb, start, stop, yup, ydn, edge, xl, xr, vf, share, held, part, parts, fin,
    load_sem, halo_send, halo_recv, part_send, part_recv, fin_send, fin_recv,
):
    samples, ny, nx = vol.shape
    half = ny // 2
    chunks = ny // each
    lag = LAG_ROWS // each
    tx, ty, me = lax.axis_index("tx"), lax.axis_index("ty"), lax.axis_index("depth")

    loads = [
        pltpu.make_async_copy(vol, vb.at[pl.ds(1, samples)], load_sem.at[0]),
        pltpu.make_async_copy(start_hbm.at[0], start, load_sem.at[1]),
        pltpu.make_async_copy(stop_hbm.at[0], stop, load_sem.at[2]),
    ]
    for load in loads:
        load.start()

    barrier = pltpu.get_barrier_semaphore()
    for rel in range(1, n):
        pl.semaphore_signal(barrier, inc=1, device_id={"depth": lax.rem(me + rel, n)}, device_id_type=MESH)
    sides = (("tx", tx, n_tx), ("ty", ty, n_ty))
    expected = n - 1
    for axis, at, count in sides:
        @pl.when(at > 0)
        def _(axis=axis, at=at):
            pl.semaphore_signal(barrier, inc=1, device_id={axis: at - 1}, device_id_type=MESH)

        @pl.when(at < count - 1)
        def _(axis=axis, at=at):
            pl.semaphore_signal(barrier, inc=1, device_id={axis: at + 1}, device_id_type=MESH)

        expected = expected + jnp.where(at > 0, 1, 0) + jnp.where(at < count - 1, 1, 0)
    pl.semaphore_wait(barrier, expected)

    def shift(slot, axis, at, count, source, target, upward):
        return pltpu.make_async_remote_copy(
            src_ref=source, dst_ref=target, send_sem=halo_send.at[slot], recv_sem=halo_recv.at[slot],
            device_id={axis: at + 1 if upward else at - 1}, device_id_type=MESH,
        )

    last, first = pl.ds(ny - STRIP, STRIP), pl.ds(0, STRIP)
    halos = [
        (shift(0, "depth", me, n, vb.at[samples], vb.at[0], True), me, n, True, lambda: vb.at[0]),
        (shift(1, "depth", me, n, vb.at[1], vb.at[samples + 1], False), me, n, False, lambda: vb.at[samples + 1]),
        (shift(2, "ty", ty, n_ty, vb.at[pl.ds(1, samples), last], yup, True), ty, n_ty, True, lambda: yup),
        (shift(3, "ty", ty, n_ty, vb.at[pl.ds(1, samples), first], ydn, False), ty, n_ty, False, lambda: ydn),
        (shift(4, "tx", tx, n_tx, edge, xl, True), tx, n_tx, True, lambda: xl),
        (shift(5, "tx", tx, n_tx, edge, xr, False), tx, n_tx, False, lambda: xr),
    ]

    def send_halo(entry):
        copy, at, count, upward, place = entry
        pl.when(at < count - 1 if upward else at > 0)(copy.start)

        @pl.when(at == 0 if upward else at == count - 1)
        def _():
            place()[...] = jnp.zeros(place().shape, jnp.bfloat16)

    loads[0].wait()
    for entry in halos[:4]:
        send_halo(entry)

    group = 4
    r = lax.broadcasted_iota(jnp.int32, (nx, nx), 0)
    c = lax.broadcasted_iota(jnp.int32, (nx, nx), 1)

    def gather(step, total):
        z0 = step * group
        hits = []
        for k in range(group):
            lane = 2 * (z0 + k)
            hit = ((r == nx - 1) & (c == lane)) | ((r == 0) & (c == lax.rem(lane + nx - 1, nx)))
            hits.append(hit.astype(jnp.float32).astype(jnp.bfloat16))
        layers = jnp.concatenate([vb[1 + z0 + k] for k in range(group)], axis=1)
        return total + dot(layers, jnp.concatenate(hits, axis=0))

    columns = lax.fori_loop(0, samples // group, gather, jnp.zeros((ny, nx), jnp.float32))
    edge[...] = (columns[:half] + pltpu.roll(columns[half:], nx // 2, 1)).astype(jnp.bfloat16)
    for entry in halos[4:]:
        send_halo(entry)

    body = pl.ds(8, ny)

    loads[1].wait()
    loads[2].wait()
    rows_each = ny // pattern.shape[1]
    slopes = [transfer[0, i] * 0.5 for i in range(3)]
    offsets = [transfer[1, i] * 0.5 for i in range(3)]
    slope, offset = transfer[0, 3] * LOG2E, transfer[1, 3] * LOG2E

    rank = [sum(jnp.where(order[q] == s, q, 0) for q in range(n)) for s in range(n)]
    before = [[jnp.where(rank[a] < rank[b], 1.0, 0.0) for b in range(n)] for a in range(n)]

    def owner_of(j):
        turn = lax.rem(j, n)
        return jnp.where(lax.rem(turn, 2) == 0, turn // 2, n - 1 - turn // 2)

    @pl.loop(0, chunks)
    def _(j):
        r0 = pl.multiple_of(j * each, each)
        rows, inner = pl.ds(r0, each), pl.ds(pl.multiple_of(r0 + 8, 8), each)
        begin = start[rows]
        end = stop[rows]
        blocks = []
        for b in range(each // rows_each):
            on = pattern[0, j * (each // rows_each) + b]
            blocks.append(jnp.where(on > 0, end[b * rows_each:(b + 1) * rows_each], 0))
        end = jnp.concatenate(blocks, axis=0)

        def layer(z, passed):
            v = vb[z + 1, rows].astype(jnp.float32)
            vf[z + 1, inner] = v
            log = jnp.log(1.0 + jnp.exp2(v * slope + offset))
            through = jnp.exp2(log * (-scale * LOG2E))
            active = (begin <= z) & (end > z)
            now = jnp.where(active, passed * through, passed)
            share[z, rows] = passed - now
            return now

        passed = lax.fori_loop(0, samples, layer, jnp.ones((each, nx), jnp.float32), unroll=UNROLL)
        hidden = encode(1.0 - passed)
        owner, k = owner_of(j), j // n

        @pl.when(owner == me)
        def _():
            parts[me, k, 3] = hidden

        @pl.when(owner != me)
        def _():
            part[j, 3] = hidden

    for copy, at, count, upward, place in halos:
        pl.when(at < count - 1 if upward else at > 0)(copy.wait_send)
        pl.when(at > 0 if upward else at < count - 1)(copy.wait_recv)

    lane = lax.broadcasted_iota(jnp.int32, (half, nx), 1)
    held[...] = jnp.where(lax.rem(lane, 2) == 0, xl[...].astype(jnp.float32), xr[...].astype(jnp.float32))
    for z in (0, samples + 1):
        vf[z, body] = vb[z].astype(jnp.float32)

    @pl.loop(0, samples)
    def _(z):
        vf[1 + z, pl.ds(0, 8)] = yup[z].astype(jnp.float32)[STRIP - 8:]
        vf[1 + z, pl.ds(8 + ny, 8)] = ydn[z].astype(jnp.float32)[:8]

    def part_copy(j, k, owner):
        return pltpu.make_async_remote_copy(
            src_ref=part.at[j], dst_ref=parts.at[me, k],
            send_sem=part_send.at[j], recv_sem=part_recv.at[me, k],
            device_id={"depth": owner}, device_id_type=MESH,
        )

    def fin_copy(j, k, rel):
        return pltpu.make_async_remote_copy(
            src_ref=fin.at[k], dst_ref=out.at[:, pl.ds(pl.multiple_of(j * each, each), each)],
            send_sem=fin_send.at[k, rel - 1], recv_sem=fin_recv.at[j],
            device_id={"depth": lax.rem(me + rel, n)}, device_id_type=MESH,
        )

    def render(j):
        r0 = pl.multiple_of(j * each, each)
        rows = pl.ds(r0, each)
        def layer(z, state):
            previous, v, total, red, green, blue = state
            after = vf[z + 2, pl.ds(pl.multiple_of(r0 + 8, 8), each)]
            near = vf.at[z + 1, pl.ds(r0, each + 16)]
            dz = after - previous
            dyv = near[pl.ds(9, each)] - near[pl.ds(7, each)]
            beside = pltpu.roll(sides_of, lax.rem(nx - 2 * z, nx), 1)
            right = jnp.where(lane == nx - 1, beside, pltpu.roll(v, nx - 1, 1))
            dxv = right - jnp.where(lane == 0, beside, pltpu.roll(v, 1, 1))
            lit = jnp.abs(0.168 * dxv + 0.21 * dyv + 0.224 * dz)
            shade = 0.15 + lit * lax.rsqrt(dxv * dxv + dyv * dyv + dz * dz + 4.0)
            weight = share[z, rows] * shade
            tints = [jnp.tanh(v * slopes[i] + offsets[i]) for i in range(3)]
            return (
                v, after, total + weight,
                red + weight * tints[0], green + weight * tints[1], blue + weight * tints[2],
            )

        upper = j * each // half
        sides_of = held[pl.ds(pl.multiple_of(r0 - upper * half, each), each)]
        sides_of = pltpu.roll(sides_of, upper * (nx // 2), 1)
        lane = lax.broadcasted_iota(jnp.int32, (each, nx), 1)
        zero = jnp.zeros((each, nx), jnp.float32)
        inner = pl.ds(pl.multiple_of(r0 + 8, 8), each)
        state = (
            vf[0, inner], vf[1, inner],
            zero, zero, zero, zero,
        )
        _, _, total, red, green, blue = lax.fori_loop(0, samples, layer, state, unroll=UNROLL)
        values = [encode(x) for x in (red + total, green + total, blue + total)]
        owner, k = owner_of(j), j // n

        @pl.when(owner == me)
        def _():
            for i in range(3):
                parts[me, k, i] = values[i]

        @pl.when(owner != me)
        def _():
            for i in range(3):
                part[j, i] = values[i]
            part_copy(j, k, owner).start()

    def merge(j):
        owner, k = owner_of(j), j // n

        @pl.when(owner == me)
        def _():
            for rel in range(1, n):
                source = lax.rem(me + rel, n)
                pltpu.make_async_remote_copy(
                    src_ref=part.at[j], dst_ref=parts.at[source, k],
                    send_sem=part_send.at[j], recv_sem=part_recv.at[source, k],
                    device_id={"depth": source}, device_id_type=MESH,
                ).wait_recv()
            hidden = [decode(parts[s, k, 3]) for s in range(n)]
            remain = 1.0 - hidden[0]
            for s in range(1, n):
                remain = remain * (1.0 - hidden[s])
            colors = [jnp.zeros_like(remain)] * 3
            for s in range(n):
                prefix = jnp.ones_like(remain)
                for a in range(n):
                    if a != s:
                        prefix = prefix * (1.0 - hidden[a] * before[a][s])
                colors = [colors[i] + prefix * decode(parts[s, k, i]) for i in range(3)]
            rows = pl.ds(pl.multiple_of(j * each, each), each)
            for i, value in enumerate(colors + [1.0 - remain]):
                fin[k, i] = encode(value)
                out[i, rows] = encode(value)
            for rel in range(1, n):
                fin_copy(j, k, rel).start()

    @pl.loop(0, chunks + lag)
    def _(j):
        pl.when(j < chunks)(lambda: render(j))
        pl.when(j >= lag)(lambda: merge(j - lag))

    @pl.loop(0, chunks)
    def _(j):
        owner, k = owner_of(j), j // n

        @pl.when(owner == me)
        def _():
            for rel in range(1, n):
                fin_copy(j, k, rel).wait_send()

        @pl.when(owner != me)
        def _():
            part_copy(j, k, owner).wait_send()
            fin_copy(j, k, 1).wait_recv()


def solution(mesh):
    n, n_tx, n_ty = mesh.shape["depth"], mesh.shape["tx"], mesh.shape["ty"]

    def shards(volume, transfer, ray_start, ray_stop, pattern, depth_order):
        samples, ny, nx = volume.shape
        rows = min(32, ny // n)
        chunks = ny // rows
        owned = chunks // n
        f32, bf16, i16 = jnp.float32, jnp.bfloat16, jnp.int16
        any_space = pl.BlockSpec(memory_space=pl.ANY)
        smem = pl.BlockSpec(memory_space=pltpu.SMEM)
        dma = pltpu.SemaphoreType.DMA
        codes = pl.pallas_call(
            functools.partial(kernel, n, n_tx, n_ty, 2.0 / (samples * n), rows),
            out_shape=jax.ShapeDtypeStruct((4, ny, nx), i16),
            in_specs=[any_space, any_space, any_space, smem, smem, smem],
            out_specs=pl.BlockSpec(memory_space=pltpu.VMEM),
            scratch_shapes=[
                pltpu.VMEM((samples + 2, ny, nx), bf16),
                pltpu.VMEM((ny, nx), jnp.int32),
                pltpu.VMEM((ny, nx), jnp.int32),
                pltpu.VMEM((samples, STRIP, nx), bf16),
                pltpu.VMEM((samples, STRIP, nx), bf16),
                pltpu.VMEM((ny // 2, nx), bf16),
                pltpu.VMEM((ny // 2, nx), bf16),
                pltpu.VMEM((ny // 2, nx), bf16),
                pltpu.VMEM((samples + 2, ny + 16, nx), f32),
                pltpu.VMEM((samples, ny, nx), f32),
                pltpu.VMEM((ny // 2, nx), f32),
                pltpu.VMEM((chunks, 4, rows, nx), i16),
                pltpu.VMEM((n, owned, 4, rows, nx), i16),
                pltpu.VMEM((owned, 4, rows, nx), i16),
                dma((3,)), dma((6,)), dma((6,)),
                dma((chunks,)), dma((n, owned)), dma((owned, n - 1)), dma((chunks,)),
            ],
            compiler_params=pltpu.CompilerParams(
                collective_id=0, has_side_effects=True, vmem_limit_bytes=62 * 1024 * 1024
            ),
        )(volume, ray_start, ray_stop, pattern[:, :, 0], transfer.T, depth_order)
        return decode(codes)

    in_specs = (
        P("depth", "ty", "tx"),
        P(),
        P("depth", "ty", "tx"),
        P("depth", "ty", "tx"),
        P("depth", "ty", "tx"),
        P(),
    )
    return jax.shard_map(shards, mesh=mesh, in_specs=in_specs, out_specs=P(None, "ty", "tx"), check_vma=False)
```
